256 devices in a mesh: blk: 16 (over y, x), box: 16 (over z, core).
Axes of the slice: x: 4, y: 4, z: 8, core: 2. Of those that a mesh axis runs over, the one named last changes fastest.
Arguments:
- excitation: bfloat16 [16, 32, 1024, 512], P('blk', 'box'), may hold values from -6 to 6
- leaf_basis: bfloat16 [16, 32, 384, 1024], P('blk', 'box'), may hold values from -0.1875 to 0.1875
- transfer: bfloat16 [16, 5, 32, 384, 768], P('blk', None, 'box'), may hold values from -0.21875 to 0.21875
- transfer_index: int32 [16, 5, 32], P('blk', None, 'box'), may hold values from 0 to 1
- out_basis: bfloat16 [16, 32, 1024, 384], P('blk', 'box'), may hold values from -0.109375 to 0.109375
Outputs:
- field: bfloat16 [32, 1024, 512], P('box', 'blk')
The draws below stay inside these ranges and needn't reach their ends.
All inputs are finite; a program needn't handle non-finite values.
Results may differ from the reference program's by a relative error of at most 0.018.
Values may be sent and summed in bfloat16 or wider, within the bound.
A program may use at most 64 MiB of HBM per device.

```python
import jax
import jax.numpy as jnp
from jax import lax

RANK = 384
COLS = 512
LEAF = 1024
OUTROWS = 1024
BOX_DEV = 2
SLOT_DEV = 2
LEVELS = 5
BLOCKS = 16
BOXES = 32
SLOTS = 32
N_BOX = 16


def touch_ends(array, own_key, least, top_value):
    longest = array.shape.index(max(array.shape))
    spots = []
    for shift in (0, 1):
        where = [jax.random.randint(jax.random.fold_in(own_key, axis), (), 0, length) for axis, length in enumerate(array.shape)]
        where[longest] = (where[longest] + shift) % array.shape[longest]
        spots.append(tuple(where))
    return array.at[spots[0]].set(least).at[spots[1]].set(top_value)


def with_spikes(values, rng, source, target, shards_of, factor):
    owner, partner = [(jnp.arange(values.shape[axis_at]) // (values.shape[axis_at] // shards_of)).reshape([-1 if axis == axis_at else 1 for axis in range(values.ndim)]) for axis_at in (source, target)]
    chosen = jax.random.permutation(rng, shards_of)[partner]
    strong = (owner == chosen) | (owner == (partner + shards_of // 2) % shards_of)
    return jnp.where(strong, factor * values, values)


def steps_of(key, shape, shards, least, largest):
    level = 1.0
    for axis_at, blocks in shards:
        draws = jax.random.uniform(jax.random.fold_in(jax.random.fold_in(key, 6), axis_at), (blocks,), jnp.float32, least / len(shards), largest / len(shards))
        level = level * jnp.repeat(jnp.exp(draws), shape[axis_at] // blocks).reshape((-1,) + (1,) * (len(shape) - 1 - axis_at))
    return level


def centred(own_key, extent, scale, reach, cuts=(), kind=jnp.bfloat16):
    array = scale * jax.random.normal(own_key, extent, jnp.float32)
    if cuts:
        array = array * steps_of(own_key, extent, cuts, -0.22, 0.18)
    return jnp.clip(array, -reach, reach).astype(kind)


def noise_with(rng, extent, width, most, cuts, heavy, kind=jnp.bfloat16):
    entries = width * jax.random.normal(rng, extent, jnp.float32)
    if cuts:
        entries = entries * steps_of(rng, extent, cuts, -0.22, 0.18)
    return jnp.clip(with_spikes(entries, jax.random.fold_in(rng, 3), *heavy), -most, most).astype(kind)


def setup_inputs(seed: int = 0) -> dict:
    keys = jax.random.split(jax.random.key(seed), 6)
    excitation = centred(keys[0], (BLOCKS, BOXES, LEAF, COLS), 1.0, 6.0, ((0, 16), (1, 16)))
    leaf_basis = centred(keys[1], (BLOCKS, BOXES, RANK, LEAF), LEAF ** -0.5, 0.1875, ((0, 16), (1, 16)))
    transfer = centred(keys[2], (BLOCKS, LEVELS, SLOTS, RANK, 2 * RANK), (2 * RANK) ** -0.5, 0.21875, ((0, 16), (2, 16)))
    transfer_index = touch_ends(jax.random.randint(keys[3], (BLOCKS, LEVELS, BOXES), 0, SLOT_DEV), jax.random.fold_in(keys[3], 1), 0, SLOT_DEV - 1).astype(jnp.int32)
    out_basis = noise_with(keys[4], (BLOCKS, BOXES, OUTROWS, RANK), (RANK * BLOCKS) ** -0.5, 0.109375, ((0, 16), (1, 16)), (0, 2, 16, 2.0))
    return {"excitation": excitation, "leaf_basis": leaf_basis, "transfer": transfer, "transfer_index": transfer_index, "out_basis": out_basis}


def one_block(total, pieces):
    excite, leaves, blocks, index, basis = pieces
    coeff = jnp.einsum('brp,bpc->brc', leaves.astype(jnp.float32), excite.astype(jnp.float32)).astype(jnp.bfloat16)
    boxes = jnp.arange(BOXES, dtype=jnp.int32)
    nbits = N_BOX.bit_length() - 1
    for level in range(LEVELS):
        if level == 0:
            mask = 1
        else:
            mask = BOX_DEV * 2 ** ((level - 1) % nbits)
        partner = jnp.bitwise_xor(boxes, mask)
        lower = (jnp.bitwise_and(boxes, mask) == 0)[:, None, None]
        other = coeff[partner]
        first = jnp.where(lower, coeff, other)
        second = jnp.where(lower, other, coeff)
        slot = (boxes // BOX_DEV) * SLOT_DEV + index[level]
        chosen = blocks[level][slot].astype(jnp.float32)
        mixed = jnp.einsum('brs,bsc->brc', chosen[:, :, :RANK], first.astype(jnp.float32))
        mixed = mixed + jnp.einsum('brs,bsc->brc', chosen[:, :, RANK:], second.astype(jnp.float32))
        coeff = mixed.astype(jnp.bfloat16)
    term = jnp.einsum('bqr,brc->bqc', basis.astype(jnp.float32), coeff.astype(jnp.float32))
    return total + term, None


def reference(excitation, leaf_basis, transfer, transfer_index, out_basis):
    start = jnp.zeros((BOXES, OUTROWS, COLS), jnp.float32)
    total, unused = lax.scan(one_block, start, (excitation, leaf_basis, transfer, transfer_index, out_basis))
    return total.astype(jnp.bfloat16)
```

```python
import jax
import jax.numpy as jnp
from jax import lax
from jax.experimental import pallas as pl
from jax.experimental.pallas import tpu as pltpu
from jax.sharding import PartitionSpec as P

MESH = pl.DeviceIdType.MESH
WIDTH = 128


def kernel(
    n_blk, n_box, index, ex_hbm, leaf_hbm, tr_hbm, ob_hbm, out, ex, leaf, tr, ob, zero, pair, share, got,
    in_sem, send_sem, recv_sem, share_sem, got_sem,
):
    chunks, boxes, rank, width = zero.shape
    items = chunks * boxes
    levels = len(tr)
    rows = share.shape[2]
    blk, me = lax.axis_index("blk"), lax.axis_index("box")
    bits = [None] + [lax.rem(me // 2 ** (level - 1), 2) for level in range(1, levels)]
    partners = [None] + [
        {"blk": blk, "box": me + 2 ** (level - 1) * (1 - 2 * bits[level])} for level in range(1, levels)
    ]

    def plane(step):
        return {"blk": lax.rem(blk + step, n_blk), "box": me}

    barrier = pltpu.get_barrier_semaphore()
    for device in partners[1:]:
        pl.semaphore_signal(barrier, inc=1, device_id=device, device_id_type=MESH)

    @pl.loop(1, n_blk)
    def _(step):
        pl.semaphore_signal(barrier, inc=1, device_id=plane(step), device_id_type=MESH)

    def columns(chunk):
        return pl.ds(pl.multiple_of(chunk * width, width), width)

    leaf_copy = pltpu.make_async_copy(leaf_hbm.at[0], leaf, in_sem.at[0])
    ex_copies = [
        pltpu.make_async_copy(ex_hbm.at[0, :, :, columns(chunk)], ex.at[chunk], in_sem.at[1 + chunk])
        for chunk in range(chunks)
    ]
    tr_copies = [
        pltpu.make_async_copy(tr_hbm.at[0, level], tr[level], in_sem.at[1 + chunks + level])
        for level in range(levels)
    ]
    ob_copy = pltpu.make_async_copy(ob_hbm.at[0], ob, in_sem.at[1 + chunks + levels])
    leaf_copy.start()
    ex_copies[0].start()
    tr_copies[0].start()
    ex_copies[1].start()
    tr_copies[1].start()
    for copy in ex_copies[2:] + tr_copies[2:] + [ob_copy]:
        copy.start()

    def mixed(level, box, both):
        matrix = tr[level][index[0, box, level]]
        return jnp.dot(matrix, both, preferred_element_type=jnp.float32).astype(jnp.bfloat16)

    def exchange(level, item):
        mine = pair[level].at[item, bits[level]]
        return pltpu.make_async_remote_copy(
            mine, mine, send_sem.at[level, item], recv_sem.at[level, item],
            device_id=partners[level], device_id_type=MESH,
        )

    def combine(level, item, box):
        exchange(level, item).wait_recv()
        return mixed(level, box, pair[level][item].reshape(2 * rank, width))

    def project(chunk):
        ex_copies[chunk].wait()
        for box in range(boxes):
            zero[chunk, box] = jnp.dot(
                leaf[box], ex[chunk, box], preferred_element_type=jnp.float32
            ).astype(jnp.bfloat16)
        if chunk == 0:
            tr_copies[0].wait()
        for box in range(boxes):
            pair[1][chunk * boxes + box, bits[1]] = mixed(0, box, zero[chunk].reshape(2 * rank, width))
        if chunk == 0:
            pl.semaphore_wait(barrier, levels - 1 + n_blk - 1)
        for box in range(boxes):
            exchange(1, chunk * boxes + box).start()

    def first(chunk):
        if chunk == 0:
            tr_copies[1].wait()
        for box in range(boxes):
            item = chunk * boxes + box
            pair[2][item, bits[2]] = combine(1, item, box)
            exchange(2, item).start()

    leaf_copy.wait()
    project(0)
    for chunk in range(1, chunks):
        project(chunk)
        first(chunk - 1)
    first(chunks - 1)

    for level in range(2, levels - 1):
        tr_copies[level].wait()

        @pl.loop(0, items)
        def _(item):
            pair[level + 1][item, bits[level + 1]] = combine(level, item, lax.rem(item, boxes))
            exchange(level + 1, item).start()

    def everyone(item, sem):
        return pltpu.make_async_copy(got.at[item], got.at[item], sem.at[item])

    def finish(item):
        everyone(item, got_sem).wait()
        total = share[item, blk].astype(jnp.float32)
        for step in range(n_blk - 1):
            total = total + got[item, step].astype(jnp.float32)
        out[lax.rem(item, boxes), :, columns(item // boxes)] = total.astype(jnp.bfloat16)

    tr_copies[levels - 1].wait()
    ob_copy.wait()

    @pl.loop(0, items)
    def _(item):
        box = lax.rem(item, boxes)
        coeff = combine(levels - 1, item, box)
        term = jnp.dot(ob[box], coeff, preferred_element_type=jnp.float32).astype(jnp.bfloat16)
        share[item] = term.reshape(n_blk, rows, width)

        @pl.loop(1, n_blk)
        def _(step):
            pltpu.make_async_remote_copy(
                share.at[item, lax.rem(blk + step, n_blk)], got.at[item, step - 1],
                share_sem.at[item], got_sem.at[item], device_id=plane(step), device_id_type=MESH,
            ).start()

        @pl.when(item >= 2)
        def _():
            finish(item - 2)

    finish(items - 2)
    finish(items - 1)

    @pl.loop(0, items)
    def _(item):
        for level in range(1, levels):
            exchange(level, item).wait_send()
        everyone(item, share_sem).wait()


def on_device(n_blk, n_box, excitation, leaf_basis, transfer, transfer_index, out_basis):
    boxes, leaf_points, columns = excitation.shape[1:]
    rank = leaf_basis.shape[2]
    levels = transfer.shape[1]
    points = out_basis.shape[2]
    chunks, rows = columns // WIDTH, points // n_blk
    items = chunks * boxes
    bf16 = jnp.bfloat16
    dma = pltpu.SemaphoreType.DMA
    hbm = pl.BlockSpec(memory_space=pl.ANY)

    def body(index, ex_hbm, leaf_hbm, tr_hbm, ob_hbm, out, *scratch):
        ex, leaf, ob, zero, share, got, in_sem, send_sem, recv_sem, share_sem, got_sem, *rest = scratch
        kernel(
            n_blk, n_box, index, ex_hbm, leaf_hbm, tr_hbm, ob_hbm, out, ex, leaf, rest[:levels], ob, zero,
            [None] + rest[levels:], share, got, in_sem, send_sem, recv_sem, share_sem, got_sem,
        )

    return pl.pallas_call(
        body,
        out_shape=jax.ShapeDtypeStruct((boxes, rows, columns), bf16),
        in_specs=[pl.BlockSpec(memory_space=pltpu.SMEM), hbm, hbm, hbm, hbm],
        out_specs=pl.BlockSpec(memory_space=pltpu.VMEM),
        scratch_shapes=[
            pltpu.VMEM((chunks, boxes, leaf_points, WIDTH), bf16),
            pltpu.VMEM((boxes, rank, leaf_points), bf16),
            pltpu.VMEM((boxes, points, rank), bf16),
            pltpu.VMEM((chunks, boxes, rank, WIDTH), bf16),
            pltpu.VMEM((items, n_blk, rows, WIDTH), bf16),
            pltpu.VMEM((items, n_blk - 1, rows, WIDTH), bf16),
            dma((chunks + levels + 2,)),
            dma((levels, items)),
            dma((levels, items)),
            dma((items,)),
            dma((items,)),
        ]
        + [pltpu.VMEM((transfer.shape[2], rank, 2 * rank), bf16) for _ in range(levels)]
        + [pltpu.VMEM((items, 2, rank, WIDTH), bf16) for _ in range(levels - 1)],
        compiler_params=pltpu.CompilerParams(
            collective_id=0, has_side_effects=True, vmem_limit_bytes=60 * 2**20
        ),
    )(jnp.swapaxes(transfer_index, 1, 2), excitation, leaf_basis, transfer, out_basis)


def solution(mesh):
    in_specs = (
        P("blk", "box", None, None),
        P("blk", "box", None, None),
        P("blk", None, "box", None, None),
        P("blk", None, "box"),
        P("blk", "box", None, None),
    )

    def step(*arrays):
        return on_device(mesh.shape["blk"], mesh.shape["box"], *arrays)

    return jax.shard_map(
        step, mesh=mesh, in_specs=in_specs, out_specs=P("box", "blk", None), check_vma=False
    )
```

```python
import functools
import math

import jax
import jax.numpy as jnp
from jax import lax
from jax.experimental import pallas as pl
from jax.experimental.pallas import tpu as pltpu
from jax.sharding import PartitionSpec as P

MESH = pl.DeviceIdType.MESH
WIDTH = 128
OUTER = (0, 5, 8, 13, 15)
INNER = (6, -2, 6, 9, 11)


def kernel(
    n_blk, n_box, index, ex_hbm, leaf_hbm, tr_hbm, ob_hbm, out, ex, leaf, tr, ob, zero, pair, share, got, line,
    in_sem, send_sem, recv_sem, share_sem, got_sem, line_sem, ends_sem, own_sem,
):
    chunks, boxes, rank, width = zero.shape
    items = chunks * boxes
    levels = len(tr)
    rows = share.shape[4]
    blk, me = lax.axis_index("blk"), lax.axis_index("box")
    bits = [None] + [lax.rem(me // 2 ** (level - 1), 2) for level in range(1, levels)]
    partners = [None] + [
        {"blk": blk, "box": me + 2 ** (level - 1) * (1 - 2 * bits[level])} for level in range(1, levels)
    ]

    side = share.shape[2]
    place = [lax.rem(blk, side), blk // side]

    def peer(along, step):
        there = lax.rem(place[along] + step, side)
        return {"blk": place[1] * side + there if along == 0 else there * side + place[0], "box": me}

    def columns(chunk):
        return pl.ds(pl.multiple_of(chunk * width, width), width)

    leaf_copy = pltpu.make_async_copy(leaf_hbm.at[0], leaf, in_sem.at[0])
    ex_copies = [
        pltpu.make_async_copy(ex_hbm.at[0, :, :, columns(chunk)], ex.at[chunk], in_sem.at[1 + chunk])
        for chunk in range(chunks)
    ]
    tr_copies = [
        pltpu.make_async_copy(tr_hbm.at[0, level], tr[level], in_sem.at[1 + chunks + level])
        for level in range(levels)
    ]
    ob_copy = pltpu.make_async_copy(ob_hbm.at[0], ob, in_sem.at[1 + chunks + levels])
    leaf_copy.start()
    ex_copies[0].start()
    tr_copies[0].start()
    barrier = pltpu.get_barrier_semaphore()
    for device in partners[1:]:
        pl.semaphore_signal(barrier, inc=1, device_id=device, device_id_type=MESH)

    for along in range(2):
        for step in range(1, side):
            pl.semaphore_signal(barrier, inc=1, device_id=peer(along, step), device_id_type=MESH)

    def mixed(level, box, both):
        matrix = tr[level][index[0, box, level]]
        return jnp.dot(matrix, both, preferred_element_type=jnp.float32).astype(jnp.bfloat16)

    def exchange(level, item):
        mine = pair[level].at[item, bits[level]]
        return pltpu.make_async_remote_copy(
            mine, mine, send_sem.at[level, item], recv_sem.at[level, item],
            device_id=partners[level], device_id_type=MESH,
        )

    def arrive(level, item):
        exchange(level, item).wait_recv()

    def combine(level, item, box):
        return mixed(level, box, pair[level][item].reshape(2 * rank, width))

    def project(chunk):
        ex_copies[chunk].wait()
        if chunk == 0:
            for copy in [ex_copies[1], tr_copies[1]] + ex_copies[2:] + tr_copies[2:] + [ob_copy]:
                copy.start()
        for box in range(boxes):
            zero[chunk, box] = jnp.dot(
                leaf[box], ex[chunk, box], preferred_element_type=jnp.float32
            ).astype(jnp.bfloat16)
        if chunk == 0:
            tr_copies[0].wait()
        for box in range(boxes):
            pair[1][chunk * boxes + box, bits[1]] = mixed(0, box, zero[chunk].reshape(2 * rank, width))
        if chunk == 0:
            pl.semaphore_wait(barrier, levels - 1 + 2 * (side - 1))
        for box in range(boxes):
            exchange(1, chunk * boxes + box).start()

    def first(chunk):
        if chunk == 0:
            tr_copies[1].wait()
        for box in range(boxes):
            item = chunk * boxes + box
            arrive(1, item)
            pair[2][item, bits[2]] = combine(1, item, box)
            exchange(2, item).start()

    def all_of(buffer, item, sem):
        return pltpu.make_async_copy(buffer.at[item], buffer.at[item], sem.at[item])

    def spot(item, half):
        return lax.rem(item, boxes), pl.ds(half * rows, rows), columns(item // boxes)

    def own(item, half):
        return pltpu.make_async_copy(
            line.at[item, half, place[1 - half]], out.at[(0, *spot(item, half))], own_sem.at[half, item]
        )

    def ends(item, sem):
        landed = out.at[1:side, lax.rem(item, boxes), :, columns(item // boxes)]
        return pltpu.make_async_copy(landed, landed, sem.at[item])

    def middle(level, item):
        if level == 2:
            arrive(level, item)
        pair[level + 1][item, bits[level + 1]] = combine(level, item, lax.rem(item, boxes))
        exchange(level + 1, item).start()

    def last(item):
        box = lax.rem(item, boxes)
        arrive(levels - 1, item)
        coeff = combine(levels - 1, item, box)
        term = jnp.dot(ob[box], coeff, preferred_element_type=jnp.float32).astype(jnp.bfloat16)
        for y in range(side):
            for x in range(side):
                for half in range(2):
                    start = ((y * side + x) * 2 + half) * rows
                    share[item, half, (x, y)[half], (y, x)[half]] = term[start : start + rows]
        for half in range(2):
            for step in range(1, side):
                pltpu.make_async_remote_copy(
                    share.at[item, half, lax.rem(place[half] + step, side)], got.at[item, half, step - 1],
                    share_sem.at[item], got_sem.at[item], device_id=peer(half, step), device_id_type=MESH,
                ).start()

    def gather(item):
        all_of(got, item, got_sem).wait()
        for half in range(2):
            total = share[item, half, place[half]].astype(jnp.float32)
            for step in range(side - 1):
                total = total + got[item, half, step].astype(jnp.float32)
            line[item, half] = total.astype(jnp.bfloat16)
            own(item, half).start()
            for step in range(1, side):
                pltpu.make_async_remote_copy(
                    line.at[item, half, lax.rem(place[1 - half] + step, side)], out.at[(step, *spot(item, half))],
                    line_sem.at[item], ends_sem.at[item], device_id=peer(1 - half, step), device_id_type=MESH,
                ).start()

    stages = [functools.partial(arrive, 3), functools.partial(middle, 2), functools.partial(middle, 3), last, gather]
    inner = lax.rem((bits[2] + bits[3]), 2)
    lags = [outer + inner * (within - outer) for outer, within in zip(OUTER, INNER)]

    def advance(step):
        for stage, lag in zip(stages, lags):

            @pl.when((step >= lag) & (step < lag + items))
            def _():
                stage(step - lag)

    leaf_copy.wait()
    project(0)
    for chunk in range(1, chunks):
        project(chunk)
        first(chunk - 1)
    for copy in tr_copies[2:] + [ob_copy]:
        copy.wait()
    advance(-2)
    first(chunks - 1)
    advance(-1)

    @pl.loop(0, items + max(OUTER + INNER))
    def _(step):
        advance(step)

    @pl.loop(0, items)
    def _(item):
        for level in range(1, levels):
            exchange(level, item).wait_send()
        all_of(got, item, share_sem).wait()
        ends(item, line_sem).wait()
        ends(item, ends_sem).wait()
        for half in range(2):
            own(item, half).wait()


def on_device(n_blk, n_box, excitation, leaf_basis, transfer, transfer_index, out_basis):
    boxes, leaf_points, columns = excitation.shape[1:]
    rank = leaf_basis.shape[2]
    levels = transfer.shape[1]
    points = out_basis.shape[2]
    chunks, rows = columns // WIDTH, points // n_blk
    side = math.isqrt(n_blk)
    items = chunks * boxes
    bf16 = jnp.bfloat16
    dma = pltpu.SemaphoreType.DMA
    hbm = pl.BlockSpec(memory_space=pl.ANY)

    def body(index, ex_hbm, leaf_hbm, tr_hbm, ob_hbm, out, *scratch):
        ex, leaf, ob, zero, *rest = scratch
        tr, pair, rest = rest[:levels], [None] + rest[levels : 2 * levels - 1], rest[2 * levels - 1 :]
        kernel(n_blk, n_box, index, ex_hbm, leaf_hbm, tr_hbm, ob_hbm, out, ex, leaf, tr, ob, zero, pair, *rest)

    terms = pl.pallas_call(
        body,
        out_shape=jax.ShapeDtypeStruct((side, boxes, rows, columns), bf16),
        in_specs=[pl.BlockSpec(memory_space=pltpu.SMEM), hbm, hbm, hbm, hbm],
        out_specs=hbm,
        scratch_shapes=[
            pltpu.VMEM((chunks, boxes, leaf_points, WIDTH), bf16),
            pltpu.VMEM((boxes, rank, leaf_points), bf16),
            pltpu.VMEM((boxes, points, rank), bf16),
            pltpu.VMEM((chunks, boxes, rank, WIDTH), bf16),
        ]
        + [pltpu.VMEM((transfer.shape[2], rank, 2 * rank), bf16) for _ in range(levels)]
        + [pltpu.VMEM((items, 2, rank, WIDTH), bf16) for _ in range(levels - 1)]
        + [
            pltpu.VMEM((items, 2, side, side, rows // 2, WIDTH), bf16),
            pltpu.VMEM((items, 2, side - 1, side, rows // 2, WIDTH), bf16),
            pltpu.VMEM((items, 2, side, rows // 2, WIDTH), bf16),
            dma((chunks + levels + 2,)),
            dma((levels, items)),
            dma((levels, items)),
        ]
        + [dma((items,)) for _ in range(4)]
        + [dma((2, items))],
        compiler_params=pltpu.CompilerParams(
            collective_id=0, has_side_effects=True, vmem_limit_bytes=60 * 2**20
        ),
    )(jnp.swapaxes(transfer_index, 1, 2), excitation, leaf_basis, transfer, out_basis)
    return sum(terms[step].astype(jnp.float32) for step in range(side)).astype(bf16)


def solution(mesh):
    in_specs = (
        P("blk", "box", None, None),
        P("blk", "box", None, None),
        P("blk", None, "box", None, None),
        P("blk", None, "box"),
        P("blk", "box", None, None),
    )

    def step(*arrays):
        return on_device(mesh.shape["blk"], mesh.shape["box"], *arrays)

    return jax.shard_map(
        step, mesh=mesh, in_specs=in_specs, out_specs=P("box", "blk", None), check_vma=False
    )
```

```python
import functools
import math

import jax
import jax.numpy as jnp
from jax import lax
from jax.experimental import pallas as pl
from jax.experimental.pallas import tpu as pltpu
from jax.sharding import PartitionSpec as P

MESH = pl.DeviceIdType.MESH
WIDTH = 128
OUTER = (0, 5, 8, 13, 15)
INNER = (6, -2, 6, 9, 11)


def kernel(
    n_blk, n_box, index_hbm, ex_hbm, leaf_hbm, tr_hbm, ob_hbm, out, ex, leaf, tr, ob, zero, pair, share, got, line,
    index, in_sem, send_sem, recv_sem, got_sem, last_sem,
):
    chunks, boxes, rank, width = zero.shape
    items = chunks * boxes
    levels = len(tr)
    rows = share.shape[4]
    blk, me = lax.axis_index("blk"), lax.axis_index("box")
    bits = [None] + [lax.rem(me // 2 ** (level - 1), 2) for level in range(1, levels)]
    partners = [None] + [
        {"blk": blk, "box": me + 2 ** (level - 1) * (1 - 2 * bits[level])} for level in range(1, levels)
    ]

    side = share.shape[2]
    place = [lax.rem(blk, side), blk // side]

    def peer(along, step):
        there = lax.rem(place[along] + step, side)
        return {"blk": place[1] * side + there if along == 0 else there * side + place[0], "box": me}

    def columns(chunk):
        return pl.ds(pl.multiple_of(chunk * width, width), width)

    leaf_copies = [pltpu.make_async_copy(leaf_hbm.at[0, box], leaf.at[box], in_sem.at[box]) for box in range(boxes)]
    ex_firsts = [
        pltpu.make_async_copy(ex_hbm.at[0, box, :, columns(0)], ex.at[0, box], in_sem.at[boxes + box])
        for box in range(boxes)
    ]
    spare = 2 * boxes - 1
    ex_copies = [None] + [
        pltpu.make_async_copy(ex_hbm.at[0, :, :, columns(chunk)], ex.at[chunk], in_sem.at[spare + chunk])
        for chunk in range(1, chunks)
    ]
    tr_copies = [
        pltpu.make_async_copy(tr_hbm.at[0, level], tr[level], in_sem.at[spare + chunks + level])
        for level in range(levels)
    ]
    ob_copy = pltpu.make_async_copy(ob_hbm.at[0], ob, in_sem.at[spare + chunks + levels])
    index_copy = pltpu.make_async_copy(index_hbm, index, in_sem.at[spare + chunks + levels + 1])
    for box in range(boxes):
        leaf_copies[box].start()
        ex_firsts[box].start()
    index_copy.start()
    tr_copies[0].start()
    barrier = pltpu.get_barrier_semaphore()
    for device in partners[1:]:
        pl.semaphore_signal(barrier, inc=1, device_id=device, device_id_type=MESH)

    for along in range(2):
        for step in range(1, side):
            pl.semaphore_signal(barrier, inc=1, device_id=peer(along, step), device_id_type=MESH)

    def mixed(level, box, both):
        matrix = tr[level][index[0, box, level]]
        return jnp.dot(matrix, both, preferred_element_type=jnp.float32).astype(jnp.bfloat16)

    def exchange(level, item):
        mine = pair[level].at[item, bits[level]]
        return pltpu.make_async_remote_copy(
            mine, mine, send_sem.at[level - 1], recv_sem.at[level - 1, item],
            device_id=partners[level], device_id_type=MESH,
        )

    def arrive(level, item):
        exchange(level, item).wait_recv()

    def combine(level, item, box):
        return mixed(level, box, pair[level][item].reshape(2 * rank, width))

    def project(chunk):
        if chunk:
            ex_copies[chunk].wait()
        for box in range(boxes):
            if chunk == 0:
                leaf_copies[box].wait()
                ex_firsts[box].wait()
            if chunk == 0 and box == boxes - 1:
                for copy in [ex_copies[1], tr_copies[1]] + ex_copies[2:] + tr_copies[2:] + [ob_copy]:
                    copy.start()
            zero[chunk, box] = jnp.dot(
                leaf[box], ex[chunk, box], preferred_element_type=jnp.float32
            ).astype(jnp.bfloat16)
        if chunk == 0:
            tr_copies[0].wait()
            index_copy.wait()
        for box in range(boxes):
            pair[1][chunk * boxes + box, bits[1]] = mixed(0, box, zero[chunk].reshape(2 * rank, width))
        if chunk == 0:
            pl.semaphore_wait(barrier, levels - 1 + 2 * (side - 1))
        for box in range(boxes):
            exchange(1, chunk * boxes + box).start()

    def first(chunk):
        if chunk == 0:
            tr_copies[1].wait()
        for box in range(boxes):
            item = chunk * boxes + box
            arrive(1, item)
            pair[2][item, bits[2]] = combine(1, item, box)
            exchange(2, item).start()

    def all_of(buffer, sem):
        return pltpu.make_async_copy(buffer, buffer, sem)

    def spot(item, half):
        return lax.rem(item, boxes), pl.ds(half * rows, rows), columns(item // boxes)

    def own(item, half):
        return pltpu.make_async_copy(
            line.at[item, half, place[1 - half]], out.at[(0, *spot(item, half))], last_sem.at[2]
        )

    def middle(level, item):
        if level == 2:
            arrive(level, item)
        pair[level + 1][item, bits[level + 1]] = combine(level, item, lax.rem(item, boxes))
        exchange(level + 1, item).start()

    def last(item):
        box = lax.rem(item, boxes)
        arrive(levels - 1, item)
        coeff = combine(levels - 1, item, box)
        term = jnp.dot(ob[box], coeff, preferred_element_type=jnp.float32).astype(jnp.bfloat16)
        for y in range(side):
            for x in range(side):
                for half in range(2):
                    start = ((y * side + x) * 2 + half) * rows
                    share[item, half, (x, y)[half], (y, x)[half]] = term[start : start + rows]
        for half in range(2):
            for step in range(1, side):
                pltpu.make_async_remote_copy(
                    share.at[item, half, lax.rem(place[half] + step, side)], got.at[item, half, step - 1],
                    last_sem.at[0], got_sem.at[item], device_id=peer(half, step), device_id_type=MESH,
                ).start()

    def gather(item):
        all_of(got.at[item], got_sem.at[item]).wait()
        for half in range(2):
            total = share[item, half, place[half]].astype(jnp.float32)
            for step in range(side - 1):
                total = total + got[item, half, step].astype(jnp.float32)
            line[item, half] = total.astype(jnp.bfloat16)
            own(item, half).start()
            for step in range(1, side):
                pltpu.make_async_remote_copy(
                    line.at[item, half, lax.rem(place[1 - half] + step, side)], out.at[(step, *spot(item, half))],
                    last_sem.at[1], last_sem.at[3], device_id=peer(1 - half, step), device_id_type=MESH,
                ).start()

    stages = [functools.partial(arrive, 3), functools.partial(middle, 2), functools.partial(middle, 3), last, gather]
    inner = lax.rem((bits[2] + bits[3]), 2)
    lags = [outer + inner * (within - outer) for outer, within in zip(OUTER, INNER)]

    def advance(step):
        for stage, lag in zip(stages, lags):

            @pl.when((step >= lag) & (step < lag + items))
            def _():
                stage(step - lag)

    project(0)
    for chunk in range(1, chunks):
        project(chunk)
        first(chunk - 1)
    for copy in tr_copies[2:] + [ob_copy]:
        copy.wait()
    advance(-2)
    first(chunks - 1)
    advance(-1)

    @pl.loop(0, items + max(OUTER + INNER))
    def _(step):
        advance(step)

    for level in range(1, levels):
        all_of(pair[level].at[:, 0], send_sem.at[level - 1]).wait()
    all_of(got, last_sem.at[0]).wait()
    all_of(out.at[1:side], last_sem.at[1]).wait()
    all_of(out.at[0], last_sem.at[2]).wait()
    all_of(out.at[1:side], last_sem.at[3]).wait()


def on_device(n_blk, n_box, excitation, leaf_basis, transfer, transfer_index, out_basis):
    boxes, leaf_points, columns = excitation.shape[1:]
    rank = leaf_basis.shape[2]
    levels = transfer.shape[1]
    points = out_basis.shape[2]
    chunks, rows = columns // WIDTH, points // n_blk
    side = math.isqrt(n_blk)
    items = chunks * boxes
    bf16 = jnp.bfloat16
    dma = pltpu.SemaphoreType.DMA
    hbm = pl.BlockSpec(memory_space=pl.ANY)

    def body(index_hbm, ex_hbm, leaf_hbm, tr_hbm, ob_hbm, out, *scratch):
        ex, leaf, ob, zero, *rest = scratch
        tr, pair, rest = rest[:levels], [None] + rest[levels : 2 * levels - 1], rest[2 * levels - 1 :]
        kernel(n_blk, n_box, index_hbm, ex_hbm, leaf_hbm, tr_hbm, ob_hbm, out, ex, leaf, tr, ob, zero, pair, *rest)

    terms = pl.pallas_call(
        body,
        out_shape=jax.ShapeDtypeStruct((side, boxes, rows, columns), bf16),
        in_specs=[hbm, hbm, hbm, hbm, hbm],
        out_specs=hbm,
        scratch_shapes=[
            pltpu.VMEM((chunks, boxes, leaf_points, WIDTH), bf16),
            pltpu.VMEM((boxes, rank, leaf_points), bf16),
            pltpu.VMEM((boxes, points, rank), bf16),
            pltpu.VMEM((chunks, boxes, rank, WIDTH), bf16),
        ]
        + [pltpu.VMEM((transfer.shape[2], rank, 2 * rank), bf16) for _ in range(levels)]
        + [pltpu.VMEM((items, 2, rank, WIDTH), bf16) for _ in range(levels - 1)]
        + [
            pltpu.VMEM((items, 2, side, side, rows // 2, WIDTH), bf16),
            pltpu.VMEM((items, 2, side - 1, side, rows // 2, WIDTH), bf16),
            pltpu.VMEM((items, 2, side, rows // 2, WIDTH), bf16),
            pltpu.SMEM((1, boxes, levels), jnp.int32),
            dma((chunks + levels + 2 * boxes + 1,)),
            dma((levels - 1,)),
            dma((levels - 1, items)),
            dma((items,)),
            dma((4,)),
        ],
        compiler_params=pltpu.CompilerParams(
            collective_id=0, has_side_effects=True, vmem_limit_bytes=60 * 2**20
        ),
    )(jnp.swapaxes(transfer_index, 1, 2), excitation, leaf_basis, transfer, out_basis)
    return sum(terms[step].astype(jnp.float32) for step in range(side)).astype(bf16)


def solution(mesh):
    in_specs = (
        P("blk", "box", None, None),
        P("blk", "box", None, None),
        P("blk", None, "box", None, None),
        P("blk", None, "box"),
        P("blk", "box", None, None),
    )

    def step(*arrays):
        return on_device(mesh.shape["blk"], mesh.shape["box"], *arrays)

    return jax.shard_map(
        step, mesh=mesh, in_specs=in_specs, out_specs=P("box", "blk", None), check_vma=False
    )
```

```python
import functools
import math

import jax
import jax.numpy as jnp
from jax import lax
from jax.experimental import pallas as pl
from jax.experimental.pallas import tpu as pltpu
from jax.sharding import PartitionSpec as P

MESH = pl.DeviceIdType.MESH
WIDTH = 128
OUTER = "AAAAAABABABBCBCBCCBBCCDCDCDEDEDDEEDEDEEE"
INNER = "-BBBBBBBACACACACDACDACDEACDEACDEDEDEDEEE"


def kernel(
    n_blk, n_box, index_hbm, ex_hbm, leaf_hbm, tr_hbm, ob_hbm, out, ex, leaf, tr, ob, zero, pair, share, got, line,
    index, in_sem, send_sem, recv_sem, got_sem, last_sem,
):
    chunks, boxes, rank, width = zero.shape
    items = chunks * boxes
    levels = len(tr)
    rows = share.shape[4]
    blk, me = lax.axis_index("blk"), lax.axis_index("box")
    bits = [None] + [lax.rem(me // 2 ** (level - 1), 2) for level in range(1, levels)]
    partners = [None] + [
        {"blk": blk, "box": me + 2 ** (level - 1) * (1 - 2 * bits[level])} for level in range(1, levels)
    ]

    side = share.shape[2]
    place = [lax.rem(blk, side), blk // side]

    def peer(along, step):
        there = lax.rem(place[along] + step, side)
        return {"blk": place[1] * side + there if along == 0 else there * side + place[0], "box": me}

    def columns(chunk):
        return pl.ds(pl.multiple_of(chunk * width, width), width)

    leaf_copies = [pltpu.make_async_copy(leaf_hbm.at[0, box], leaf.at[box], in_sem.at[box]) for box in range(boxes)]
    ex_firsts = [
        pltpu.make_async_copy(ex_hbm.at[0, box, :, columns(0)], ex.at[0, box], in_sem.at[boxes + box])
        for box in range(boxes)
    ]
    spare = 2 * boxes - 1
    ex_copies = [None] + [
        pltpu.make_async_copy(ex_hbm.at[0, :, :, columns(chunk)], ex.at[chunk], in_sem.at[spare + chunk])
        for chunk in range(1, chunks)
    ]
    tr_copies = [
        pltpu.make_async_copy(tr_hbm.at[0, level], tr[level], in_sem.at[spare + chunks + level])
        for level in range(levels)
    ]
    ob_copy = pltpu.make_async_copy(ob_hbm.at[0], ob, in_sem.at[spare + chunks + levels])
    index_copy = pltpu.make_async_copy(index_hbm, index, in_sem.at[spare + chunks + levels + 1])
    for box in range(boxes):
        leaf_copies[box].start()
        ex_firsts[box].start()
    index_copy.start()
    tr_copies[0].start()
    barrier = pltpu.get_barrier_semaphore()
    for device in partners[1:]:
        pl.semaphore_signal(barrier, inc=1, device_id=device, device_id_type=MESH)

    for along in range(2):
        for step in range(1, side):
            pl.semaphore_signal(barrier, inc=1, device_id=peer(along, step), device_id_type=MESH)

    def mixed(level, box, both):
        matrix = tr[level][index[0, box, level]]
        return jnp.dot(matrix, both, preferred_element_type=jnp.float32).astype(jnp.bfloat16)

    def exchange(level, item):
        mine = pair[level].at[item, bits[level]]
        return pltpu.make_async_remote_copy(
            mine, mine, send_sem.at[level - 1], recv_sem.at[level - 1, item],
            device_id=partners[level], device_id_type=MESH,
        )

    def arrive(level, item):
        exchange(level, item).wait_recv()

    def combine(level, item, box):
        return mixed(level, box, pair[level][item].reshape(2 * rank, width))

    def project(chunk):
        if chunk:
            ex_copies[chunk].wait()
        for box in range(boxes):
            if chunk == 0:
                leaf_copies[box].wait()
                ex_firsts[box].wait()
            if chunk == 0 and box == boxes - 1:
                for copy in [ex_copies[1], tr_copies[1]] + ex_copies[2:] + tr_copies[2:] + [ob_copy]:
                    copy.start()
            zero[chunk, box] = jnp.dot(
                leaf[box], ex[chunk, box], preferred_element_type=jnp.float32
            ).astype(jnp.bfloat16)
        if chunk == 0:
            tr_copies[0].wait()
            index_copy.wait()
        for box in range(boxes):
            pair[1][chunk * boxes + box, bits[1]] = mixed(0, box, zero[chunk].reshape(2 * rank, width))
        if chunk == 0:
            pl.semaphore_wait(barrier, levels - 1 + 2 * (side - 1))
        for box in range(boxes):
            exchange(1, chunk * boxes + box).start()

    def first(chunk):
        if chunk == 0:
            tr_copies[1].wait()
        for box in range(boxes):
            item = chunk * boxes + box
            arrive(1, item)
            pair[2][item, bits[2]] = combine(1, item, box)
            exchange(2, item).start()

    def all_of(buffer, sem):
        return pltpu.make_async_copy(buffer, buffer, sem)

    def spot(item, half):
        return lax.rem(item, boxes), pl.ds(half * rows, rows), columns(item // boxes)

    def own(item, half):
        return pltpu.make_async_copy(
            line.at[item, half, place[1 - half]], out.at[(0, *spot(item, half))], last_sem.at[2]
        )

    def middle(level, item):
        if level == 2:
            arrive(level, item)
        pair[level + 1][item, bits[level + 1]] = combine(level, item, lax.rem(item, boxes))
        exchange(level + 1, item).start()

    def last(item):
        box = lax.rem(item, boxes)
        arrive(levels - 1, item)
        coeff = combine(levels - 1, item, box)
        term = jnp.dot(ob[box], coeff, preferred_element_type=jnp.float32).astype(jnp.bfloat16)
        for y in range(side):
            for x in range(side):
                for half in range(2):
                    start = ((y * side + x) * 2 + half) * rows
                    share[item, half, (x, y)[half], (y, x)[half]] = term[start : start + rows]
        for half in range(2):
            for step in range(1, side):
                pltpu.make_async_remote_copy(
                    share.at[item, half, lax.rem(place[half] + step, side)], got.at[item, half, step - 1],
                    last_sem.at[0], got_sem.at[item], device_id=peer(half, step), device_id_type=MESH,
                ).start()

    def gather(item):
        all_of(got.at[item], got_sem.at[item]).wait()
        for half in range(2):
            total = share[item, half, place[half]].astype(jnp.float32)
            for step in range(side - 1):
                total = total + got[item, half, step].astype(jnp.float32)
            line[item, half] = total.astype(jnp.bfloat16)
            own(item, half).start()
            for step in range(1, side):
                pltpu.make_async_remote_copy(
                    line.at[item, half, lax.rem(place[1 - half] + step, side)], out.at[(step, *spot(item, half))],
                    last_sem.at[1], last_sem.at[3], device_id=peer(1 - half, step), device_id_type=MESH,
                ).start()

    stages = [functools.partial(arrive, 3), functools.partial(middle, 2), functools.partial(middle, 3), last, gather]
    inner = lax.rem((bits[2] + bits[3]), 2)

    def codes(order, items_done):
        taken, found = dict(items_done), []
        for letter in order:
            if letter == "-":
                found.append(len(stages) * items)
                continue
            stage = "ABCDE".index(letter)
            found.append(stage * items + taken.get(stage, 0))
            taken[stage] = taken.get(stage, 0) + 1
        return found

    lists = [codes(OUTER, {}), codes(INNER, {1: 1})]
    words = [
        [sum(code << 6 * place for place, code in enumerate(found[start : start + 5])) for start in range(0, len(found), 5)]
        for found in lists
    ]
    steps = len(lists[0])

    def code_at(step):
        word = jnp.int32(0)
        for number, pair_of in enumerate(zip(*words)):
            word = jnp.where(step // 5 == number, jnp.where(inner == 1, pair_of[1], pair_of[0]), word)
        return lax.rem(lax.shift_right_logical(word, 6 * lax.rem(step, 5)), 64)

    project(0)
    for chunk in range(1, chunks):
        project(chunk)
        first(chunk - 1)
    for copy in tr_copies[2:] + [ob_copy]:
        copy.wait()

    @pl.when(inner == 1)
    def _():
        middle(2, 0)

    first(chunks - 1)

    @pl.loop(0, steps)
    def _(step):
        code = code_at(step)
        for number, stage in enumerate(stages):

            @pl.when(code // items == number)
            def _():
                stage(lax.rem(code, items))

    for level in range(1, levels):
        all_of(pair[level].at[:, 0], send_sem.at[level - 1]).wait()
    all_of(got, last_sem.at[0]).wait()
    all_of(out.at[1:side], last_sem.at[1]).wait()
    all_of(out.at[0], last_sem.at[2]).wait()
    all_of(out.at[1:side], last_sem.at[3]).wait()


def on_device(n_blk, n_box, excitation, leaf_basis, transfer, transfer_index, out_basis):
    boxes, leaf_points, columns = excitation.shape[1:]
    rank = leaf_basis.shape[2]
    levels = transfer.shape[1]
    points = out_basis.shape[2]
    chunks, rows = columns // WIDTH, points // n_blk
    side = math.isqrt(n_blk)
    items = chunks * boxes
    bf16 = jnp.bfloat16
    dma = pltpu.SemaphoreType.DMA
    hbm = pl.BlockSpec(memory_space=pl.ANY)

    def body(index_hbm, ex_hbm, leaf_hbm, tr_hbm, ob_hbm, out, *scratch):
        ex, leaf, ob, zero, *rest = scratch
        tr, pair, rest = rest[:levels], [None] + rest[levels : 2 * levels - 1], rest[2 * levels - 1 :]
        kernel(n_blk, n_box, index_hbm, ex_hbm, leaf_hbm, tr_hbm, ob_hbm, out, ex, leaf, tr, ob, zero, pair, *rest)

    terms = pl.pallas_call(
        body,
        out_shape=jax.ShapeDtypeStruct((side, boxes, rows, columns), bf16),
        in_specs=[hbm, hbm, hbm, hbm, hbm],
        out_specs=hbm,
        scratch_shapes=[
            pltpu.VMEM((chunks, boxes, leaf_points, WIDTH), bf16),
            pltpu.VMEM((boxes, rank, leaf_points), bf16),
            pltpu.VMEM((boxes, points, rank), bf16),
            pltpu.VMEM((chunks, boxes, rank, WIDTH), bf16),
        ]
        + [pltpu.VMEM((transfer.shape[2], rank, 2 * rank), bf16) for _ in range(levels)]
        + [pltpu.VMEM((items, 2, rank, WIDTH), bf16) for _ in range(levels - 1)]
        + [
            pltpu.VMEM((items, 2, side, side, rows // 2, WIDTH), bf16),
            pltpu.VMEM((items, 2, side - 1, side, rows // 2, WIDTH), bf16),
            pltpu.VMEM((items, 2, side, rows // 2, WIDTH), bf16),
            pltpu.SMEM((1, boxes, levels), jnp.int32),
            dma((chunks + levels + 2 * boxes + 1,)),
            dma((levels - 1,)),
            dma((levels - 1, items)),
            dma((items,)),
            dma((4,)),
        ],
        compiler_params=pltpu.CompilerParams(
            collective_id=0, has_side_effects=True, vmem_limit_bytes=60 * 2**20
        ),
    )(jnp.swapaxes(transfer_index, 1, 2), excitation, leaf_basis, transfer, out_basis)
    return sum(terms[step].astype(jnp.float32) for step in range(side)).astype(bf16)


def solution(mesh):
    in_specs = (
        P("blk", "box", None, None),
        P("blk", "box", None, None),
        P("blk", None, "box", None, None),
        P("blk", None, "box"),
        P("blk", "box", None, None),
    )

    def step(*arrays):
        return on_device(mesh.shape["blk"], mesh.shape["box"], *arrays)

    return jax.shard_map(
        step, mesh=mesh, in_specs=in_specs, out_specs=P("box", "blk", None), check_vma=False
    )
```

```python
import functools
import math

import jax
import jax.numpy as jnp
from jax import lax
from jax.experimental import pallas as pl
from jax.experimental.pallas import tpu as pltpu
from jax.sharding import PartitionSpec as P

MESH = pl.DeviceIdType.MESH
WIDTH = 128
OUTER = "AAAAAABABABBCBCBCCBBCCDCDCDEDEDDEEDEDEEE"
INNER = "-BBBBBBBACACACACDACDACDEACDEACDEDEDEDEEE"


def kernel(
    n_blk, n_box, index_hbm, ex_hbm, leaf_hbm, tr_hbm, ob_hbm, out, ex, leaf, tr, ob, zero, pair, share, got, line,
    index, in_sem, send_sem, recv_sem, got_sem, last_sem,
):
    chunks, boxes, rank, width = zero.shape
    items = chunks * boxes
    levels = len(tr)
    rows = share.shape[4]
    blk, me = lax.axis_index("blk"), lax.axis_index("box")
    bits = [None] + [lax.rem(me // 2 ** (level - 1), 2) for level in range(1, levels)]
    partners = [None] + [
        {"blk": blk, "box": me + 2 ** (level - 1) * (1 - 2 * bits[level])} for level in range(1, levels)
    ]

    side = share.shape[2]
    place = [lax.rem(blk, side), blk // side]

    def peer(along, step):
        there = lax.rem(place[along] + step, side)
        return {"blk": place[1] * side + there if along == 0 else there * side + place[0], "box": me}

    def columns(chunk):
        return pl.ds(pl.multiple_of(chunk * width, width), width)

    leaf_copies = [pltpu.make_async_copy(leaf_hbm.at[0, box], leaf.at[box], in_sem.at[box]) for box in range(boxes)]
    ex_firsts = [
        pltpu.make_async_copy(ex_hbm.at[0, box, :, columns(0)], ex.at[0, box], in_sem.at[boxes + box])
        for box in range(boxes)
    ]
    spare = 2 * boxes - 1
    ex_copies = [None] + [
        pltpu.make_async_copy(ex_hbm.at[0, :, :, columns(chunk)], ex.at[chunk], in_sem.at[spare + chunk])
        for chunk in range(1, chunks)
    ]
    tr_copies = [
        pltpu.make_async_copy(tr_hbm.at[0, level], tr[level], in_sem.at[spare + chunks + level])
        for level in range(levels)
    ]
    ob_copy = pltpu.make_async_copy(ob_hbm.at[0], ob, in_sem.at[spare + chunks + levels])
    index_copy = pltpu.make_async_copy(index_hbm, index, in_sem.at[spare + chunks + levels + 1])
    for box in range(boxes):
        leaf_copies[box].start()
        ex_firsts[box].start()
    index_copy.start()
    tr_copies[0].start()
    barrier = pltpu.get_barrier_semaphore()
    for device in partners[1:]:
        pl.semaphore_signal(barrier, inc=1, device_id=device, device_id_type=MESH)

    for along in range(2):
        for step in range(1, side):
            pl.semaphore_signal(barrier, inc=1, device_id=peer(along, step), device_id_type=MESH)

    def mixed(level, box, both):
        matrix = tr[level][index[0, box, level]]
        return jnp.dot(matrix, both, preferred_element_type=jnp.float32).astype(jnp.bfloat16)

    def exchange(level, item):
        mine = pair[level].at[item, bits[level]]
        return pltpu.make_async_remote_copy(
            mine, mine, send_sem.at[level - 1], recv_sem.at[level - 1, item],
            device_id=partners[level], device_id_type=MESH,
        )

    def arrive(level, item):
        exchange(level, item).wait_recv()

    def combine(level, item, box):
        return mixed(level, box, pair[level][item].reshape(2 * rank, width))

    def project(chunk):
        if chunk:
            ex_copies[chunk].wait()
        for box in range(boxes):
            if chunk == 0:
                leaf_copies[box].wait()
                ex_firsts[box].wait()
            if chunk == 0 and box == boxes - 1:
                for copy in [ex_copies[1], tr_copies[1]] + ex_copies[2:] + tr_copies[2:] + [ob_copy]:
                    copy.start()
            zero[chunk, box] = jnp.dot(
                leaf[box], ex[chunk, box], preferred_element_type=jnp.float32
            ).astype(jnp.bfloat16)
        if chunk == 0:
            tr_copies[0].wait()
            index_copy.wait()
        for box in range(boxes):
            pair[1][chunk * boxes + box, bits[1]] = mixed(0, box, zero[chunk].reshape(2 * rank, width))
        if chunk == 0:
            pl.semaphore_wait(barrier, levels - 1 + 2 * (side - 1))
        for box in range(boxes):
            exchange(1, chunk * boxes + box).start()

    def first(chunk):
        if chunk == 0:
            tr_copies[1].wait()
        for box in range(boxes):
            item = chunk * boxes + box
            arrive(1, item)
            pair[2][item, bits[2]] = combine(1, item, box)
            exchange(2, item).start()

    def all_of(buffer, sem):
        return pltpu.make_async_copy(buffer, buffer, sem)

    def spot(item, half):
        return lax.rem(item, boxes), pl.ds(half * rows, rows), columns(item // boxes)

    def own(item, half):
        return pltpu.make_async_copy(
            line.at[item, half, place[1 - half]], out.at[(0, *spot(item, half))], last_sem.at[2]
        )

    def middle(level, item):
        if level == 2:
            arrive(level, item)
        pair[level + 1][item, bits[level + 1]] = combine(level, item, lax.rem(item, boxes))
        exchange(level + 1, item).start()

    def last(item):
        box = lax.rem(item, boxes)
        arrive(levels - 1, item)
        coeff = combine(levels - 1, item, box)
        block = 2 * side * rows

        def send(half, step):
            pltpu.make_async_remote_copy(
                share.at[item, half, lax.rem(place[half] + step, side)], got.at[item, half, step - 1],
                last_sem.at[0], got_sem.at[item], device_id=peer(half, step), device_id_type=MESH,
            ).start()

        for step in list(range(1, side)) + [0]:
            y = lax.rem(place[1] + step, side)
            part = ob[box, pl.ds(pl.multiple_of(y * block, block), block)]
            term = jnp.dot(part, coeff, preferred_element_type=jnp.float32).astype(jnp.bfloat16)
            for x in range(side):
                start = 2 * x * rows
                share[item, 0, x, y] = term[start : start + rows]
                share[item, 1, y, x] = term[start + rows : start + 2 * rows]
            if step:
                send(1, step)
        for step in range(1, side):
            send(0, step)

    def gather(item):
        all_of(got.at[item], got_sem.at[item]).wait()
        for half in range(2):
            total = share[item, half, place[half]].astype(jnp.float32)
            for step in range(side - 1):
                total = total + got[item, half, step].astype(jnp.float32)
            line[item, half] = total.astype(jnp.bfloat16)
            for step in range(1, side):
                pltpu.make_async_remote_copy(
                    line.at[item, half, lax.rem(place[1 - half] + step, side)], out.at[(step, *spot(item, half))],
                    last_sem.at[1], last_sem.at[3], device_id=peer(1 - half, step), device_id_type=MESH,
                ).start()
            own(item, half).start()

    stages = [functools.partial(arrive, 3), functools.partial(middle, 2), functools.partial(middle, 3), last, gather]
    inner = lax.rem((bits[2] + bits[3]), 2)

    def codes(order, items_done):
        taken, found = dict(items_done), []
        for letter in order:
            if letter == "-":
                found.append(len(stages) * items)
                continue
            stage = "ABCDE".index(letter)
            found.append(stage * items + taken.get(stage, 0))
            taken[stage] = taken.get(stage, 0) + 1
        return found

    lists = [codes(OUTER, {}), codes(INNER, {1: 1})]
    words = [
        [sum(code << 6 * place for place, code in enumerate(found[start : start + 5])) for start in range(0, len(found), 5)]
        for found in lists
    ]
    steps = len(lists[0])

    def code_at(step):
        word = jnp.int32(0)
        for number, pair_of in enumerate(zip(*words)):
            word = jnp.where(step // 5 == number, jnp.where(inner == 1, pair_of[1], pair_of[0]), word)
        return lax.rem(lax.shift_right_logical(word, 6 * lax.rem(step, 5)), 64)

    project(0)
    for chunk in range(1, chunks):
        project(chunk)
        first(chunk - 1)
    for copy in tr_copies[2:] + [ob_copy]:
        copy.wait()

    @pl.when(inner == 1)
    def _():
        middle(2, 0)

    first(chunks - 1)

    @pl.loop(0, steps)
    def _(step):
        code = code_at(step)
        for number, stage in enumerate(stages):

            @pl.when(code // items == number)
            def _():
                stage(lax.rem(code, items))

    for level in range(1, levels):
        all_of(pair[level].at[:, 0], send_sem.at[level - 1]).wait()
    all_of(got, last_sem.at[0]).wait()
    all_of(out.at[1:side], last_sem.at[1]).wait()
    all_of(out.at[0], last_sem.at[2]).wait()
    all_of(out.at[1:side], last_sem.at[3]).wait()


def on_device(n_blk, n_box, excitation, leaf_basis, transfer, transfer_index, out_basis):
    boxes, leaf_points, columns = excitation.shape[1:]
    rank = leaf_basis.shape[2]
    levels = transfer.shape[1]
    points = out_basis.shape[2]
    chunks, rows = columns // WIDTH, points // n_blk
    side = math.isqrt(n_blk)
    items = chunks * boxes
    bf16 = jnp.bfloat16
    dma = pltpu.SemaphoreType.DMA
    hbm = pl.BlockSpec(memory_space=pl.ANY)

    def body(index_hbm, ex_hbm, leaf_hbm, tr_hbm, ob_hbm, out, *scratch):
        ex, leaf, ob, zero, *rest = scratch
        tr, pair, rest = rest[:levels], [None] + rest[levels : 2 * levels - 1], rest[2 * levels - 1 :]
        kernel(n_blk, n_box, index_hbm, ex_hbm, leaf_hbm, tr_hbm, ob_hbm, out, ex, leaf, tr, ob, zero, pair, *rest)

    terms = pl.pallas_call(
        body,
        out_shape=jax.ShapeDtypeStruct((side, boxes, rows, columns), bf16),
        in_specs=[hbm, hbm, hbm, hbm, hbm],
        out_specs=hbm,
        scratch_shapes=[
            pltpu.VMEM((chunks, boxes, leaf_points, WIDTH), bf16),
            pltpu.VMEM((boxes, rank, leaf_points), bf16),
            pltpu.VMEM((boxes, points, rank), bf16),
            pltpu.VMEM((chunks, boxes, rank, WIDTH), bf16),
        ]
        + [pltpu.VMEM((transfer.shape[2], rank, 2 * rank), bf16) for _ in range(levels)]
        + [pltpu.VMEM((items, 2, rank, WIDTH), bf16) for _ in range(levels - 1)]
        + [
            pltpu.VMEM((items, 2, side, side, rows // 2, WIDTH), bf16),
            pltpu.VMEM((items, 2, side - 1, side, rows // 2, WIDTH), bf16),
            pltpu.VMEM((items, 2, side, rows // 2, WIDTH), bf16),
            pltpu.SMEM((1, boxes, levels), jnp.int32),
            dma((chunks + levels + 2 * boxes + 1,)),
            dma((levels - 1,)),
            dma((levels - 1, items)),
            dma((items,)),
            dma((4,)),
        ],
        compiler_params=pltpu.CompilerParams(
            collective_id=0, has_side_effects=True, vmem_limit_bytes=60 * 2**20
        ),
    )(jnp.swapaxes(transfer_index, 1, 2), excitation, leaf_basis, transfer, out_basis)
    return sum(terms[step].astype(jnp.float32) for step in range(side)).astype(bf16)


def solution(mesh):
    in_specs = (
        P("blk", "box", None, None),
        P("blk", "box", None, None),
        P("blk", None, "box", None, None),
        P("blk", None, "box"),
        P("blk", "box", None, None),
    )

    def step(*arrays):
        return on_device(mesh.shape["blk"], mesh.shape["box"], *arrays)

    return jax.shard_map(
        step, mesh=mesh, in_specs=in_specs, out_specs=P("box", "blk", None), check_vma=False
    )
```
